32 devices in a mesh: front: 8 (over z, core), tile: 4 (over y, x).
Axes of the slice: x: 2, y: 2, z: 4, core: 2. Of those that a mesh axis runs over, the one named last changes fastest.
Arguments:
- child_rhs: float32 [8, 2048, 256], P('front', 'tile'), may hold values from -6 to 6
- child_lower: float32 [8, 2048, 2048], P('front', 'tile'), as said below
- child_border: float32 [8, 2048, 2048], P('front', 'tile'), may hold values from -0.125 to 0.125
- child_upper_border: float32 [8, 2048, 2048], P('front', 'tile'), may hold values from -0.125 to 0.125
- child_upper: float32 [8, 2048, 2048], P('front', 'tile'), as said below
- parent_rhs: float32 [8, 512, 256], P('front', 'tile'), may hold values from -6 to 6
- parent_lower: float32 [8, 512, 2048], P('front', 'tile'), as said below
- parent_upper: float32 [8, 512, 2048], P('front', 'tile'), as said below
- border_map: int32 [8, 2048], P('front'), may hold values from 0 to 2047, as said below
- border_count: int32 [8], P('front'), may hold values from 512 to 2048, as said below
Outputs:
- child_solution: float32 [8, 2048, 256], P('front', 'tile')
- parent_solution: float32 [8, 512, 256], P('front', 'tile')
The draws below stay inside these ranges and needn't reach their ends.
Inputs may be any that keep to these rules, and one draw needn't show every extreme that they name: `border_map`: within one child the 2048 entries are distinct parent rows. Group g of parent rows holds the rows m with (m mod (512)) // 128 = g, for g below 4. In every aligned block of 512 border rows of a child, each group receives either no row or exactly 256 rows, and each group receives 2048 // 4 border rows of the child in all. `border_count`: some child has all 2048 border rows live. `child_lower`: lower triangular including the diagonal. `child_upper`: upper triangular including the diagonal. `parent_lower`: each parent's 2048 rows form a lower triangular matrix including the diagonal. `parent_upper`: each parent's 2048 rows form an upper triangular matrix including the diagonal.
All inputs are finite; a program needn't handle non-finite values.
Results may differ from the reference program's by a relative error of at most 0.00013.
Values sent between devices are 32-bit elements; how exact they have to be, the bound alone decides.
A program may use at most 64 MiB of HBM per device.

```python
import math
import jax
import jax.numpy as jnp
from jax import lax

P_SIZE = 2048
B = 2048
PP = 2048
R = 256
FRONTS = 8
PARENTS = 2
CAP = 256
N_TILE = 4


def triangle(key, number, order, lower_side):
    first, second = jax.random.split(key)
    spread = jax.random.normal(first, (number, order, order), jnp.float32)
    spread = spread / math.sqrt(order)
    diagonal = jax.random.uniform(second, (number, order, 1), jnp.float32, 0.7, 1.4)
    row_ids = jnp.arange(order)[:, None]
    col_ids = jnp.arange(order)[None, :]
    if lower_side:
        inside = col_ids < row_ids
    else:
        inside = col_ids > row_ids
    return jnp.where(inside, spread, 0.0) + jnp.where(col_ids == row_ids, diagonal, 0.0)


def draw_child_lower(key, part):
    return triangle(jax.random.fold_in(key, 11), FRONTS, P_SIZE, True)


def draw_child_upper(key, part):
    return triangle(jax.random.fold_in(key, 12), FRONTS, P_SIZE, False)


def draw_parent_lower(key, part):
    return triangle(jax.random.fold_in(key, 13), PARENTS, PP, True).reshape(FRONTS, PP // 4, PP)


def draw_parent_upper(key, part):
    return triangle(jax.random.fold_in(key, 14), PARENTS, PP, False).reshape(FRONTS, PP // 4, PP)


def draw_border_map(key, part):
    block = B // N_TILE
    groups = block // CAP
    width = PP // N_TILE
    slab = PP // (4 * N_TILE)
    quarter_size = PP // 4
    keys = jax.random.split(jax.random.fold_in(key, 15), FRONTS)

    def single(one):
        first, second, third = jax.random.split(one, 3)
        offset = jax.random.randint(first, (), 0, N_TILE)
        slots = jax.vmap(lambda inner: jax.random.permutation(inner, width))(jax.random.split(second, N_TILE))
        source = jnp.arange(N_TILE, dtype=jnp.int32)[:, None, None]
        section = jnp.arange(groups, dtype=jnp.int32)[None, :, None]
        lane = jnp.arange(CAP, dtype=jnp.int32)[None, None, :]
        shape = (N_TILE, groups, CAP)
        target_tile = jnp.broadcast_to((source + offset + section) % N_TILE, shape)
        ordinal = jnp.broadcast_to(section * CAP + lane, shape)
        place = (target_tile * width + slots[target_tile, ordinal]).reshape(N_TILE, block)
        orders = jax.vmap(lambda inner: jax.random.permutation(inner, block))(jax.random.split(third, N_TILE))
        place = jnp.take_along_axis(place, orders, axis=1).reshape(B)
        tile_of = place // (4 * slab)
        quarter_of = place % (4 * slab) // slab
        rest = place % slab
        return (quarter_of * quarter_size + tile_of * slab + rest).astype(jnp.int32)
    return jax.vmap(single)(keys).astype(jnp.int32)


def draw_border_count(key, part):
    first, second = jax.random.split(jax.random.fold_in(key, 16))
    base_counts = jax.random.randint(first, (FRONTS,), B // 4, B + 1)
    chosen = jax.random.randint(second, (), 0, FRONTS)
    return jnp.where(jnp.arange(FRONTS) == chosen, B, base_counts).astype(jnp.int32)


def level_of(own_key, extent, cuts, low, top_value):
    loudness, own = 1.0, jax.random.fold_in(own_key, 6)
    for position, shards_of in cuts:
        draws = jnp.exp(jax.random.uniform(jax.random.fold_in(own, position), (shards_of,), jnp.float32, low / len(cuts), top_value / len(cuts)))
        loudness = loudness * jnp.repeat(draws, extent[position] // shards_of).reshape([-1 if axis == position else 1 for axis in range(len(extent))])
    return loudness


def scatter_about(key, dims, scale, bound, cuts=(), kind=jnp.bfloat16):
    result = jax.random.normal(key, dims, jnp.float32) * scale
    if len(cuts) > 0:
        result = level_of(key, dims, cuts, -0.22, 0.18) * result
    return jnp.clip(result, min=-bound, max=bound).astype(kind)


def setup_inputs(seed: int = 0) -> dict:
    streams_of = jax.random.split(jax.random.key(seed), 11)
    return {
        "child_rhs": scatter_about(streams_of[0], (FRONTS, P_SIZE, R), 1.0, 6.0, ((0, 8), (1, 4)), jnp.float32),
        "child_lower": draw_child_lower(jax.random.fold_in(streams_of[10], 71), 0),
        "child_border": scatter_about(streams_of[2], (FRONTS, B, P_SIZE), P_SIZE ** -0.5, 0.125, ((0, 8), (1, 4)), jnp.float32),
        "child_upper_border": scatter_about(streams_of[3], (FRONTS, P_SIZE, B), B ** -0.5, 0.125, ((0, 8), (1, 4)), jnp.float32),
        "child_upper": draw_child_upper(jax.random.fold_in(streams_of[10], 71), 0),
        "parent_rhs": scatter_about(streams_of[5], (FRONTS, PP // 4, R), 1.0, 6.0, ((0, 8), (1, 4)), jnp.float32),
        "parent_lower": draw_parent_lower(jax.random.fold_in(streams_of[10], 71), 0),
        "parent_upper": draw_parent_upper(jax.random.fold_in(streams_of[10], 71), 0),
        "border_map": draw_border_map(jax.random.fold_in(streams_of[10], 71), 0),
        "border_count": draw_border_count(jax.random.fold_in(streams_of[10], 71), 0),
    }


def reference(child_rhs, child_lower, child_border, child_upper_border, child_upper, parent_rhs, parent_lower, parent_upper, border_map, border_count):
    highest = lax.Precision.HIGHEST
    forward_child = jnp.einsum('cij,cjr->cir', child_lower, child_rhs, precision=highest)
    alive_rows = jnp.arange(B, dtype=jnp.int32)[None, :] < border_count[:, None]
    update = -jnp.einsum('cij,cjr->cir', child_border, forward_child, precision=highest)
    update = jnp.where(alive_rows[:, :, None], update, jnp.zeros_like(update))
    owners = (jnp.arange(FRONTS, dtype=jnp.int32) // 4).astype(jnp.int32)
    owner_grid = jnp.broadcast_to(owners[:, None], border_map.shape)
    gathered = jnp.zeros((PARENTS, PP, R), update.dtype).at[owner_grid, border_map].add(update)
    right_parent = parent_rhs.reshape(PARENTS, PP, R) + gathered
    forward_parent = jnp.einsum('kij,kjr->kir', parent_lower.reshape(PARENTS, PP, PP), right_parent, precision=highest)
    solved_parent = jnp.einsum('kij,kjr->kir', parent_upper.reshape(PARENTS, PP, PP), forward_parent, precision=highest)
    picked = solved_parent[owner_grid, border_map]
    border_values = jnp.where(alive_rows[:, :, None], picked, jnp.zeros_like(picked))
    reduced = forward_child - jnp.einsum('cij,cjr->cir', child_upper_border, border_values, precision=highest)
    child_solution = jnp.einsum('cij,cjr->cir', child_upper, reduced, precision=highest)
    return child_solution, solved_parent.reshape(FRONTS, PP // 4, R)
```

```python
import functools

import jax
import jax.numpy as jnp
from jax import lax
from jax.experimental import pallas as pl
from jax.experimental.pallas import tpu as pltpu
from jax.sharding import PartitionSpec as P

F32 = jnp.float32
BF16 = jnp.bfloat16


def split(x):
    high = x.astype(BF16)
    return high, (x - high.astype(F32)).astype(BF16)


def dot(a, b):
    return jnp.dot(a, b, preferred_element_type=F32)


def dot3(a, b):
    ah, al = a
    bh, bl = b
    return dot(ah, bh) + (dot(ah, bl) + dot(al, bh))


def cut_rows(rows, parts):
    units = rows // 8
    sizes = [8 * (units // parts + (1 if p < units % parts else 0)) for p in range(parts)]
    starts = [sum(sizes[:p]) for p in range(parts)]
    return list(zip(starts, sizes))


def rotate(items, by):
    by %= len(items)
    return items[by:] + items[:by]


def kernel(
    tile_bits,
    rhs_hbm, lower_hbm, border_hbm, ub_hbm, upper_hbm, prhs_ref, plower_hbm, pupper_hbm,
    map_ref, count_ref,
    child_out, parent_out,
    rhs_buf, fc_buf, red_buf, p1, p2, p3, part, landing,
    lower, border, ub, upper, plower, pupper, ub_high, ub_low, ubp_high, ubp_low,
    send_sems, recv_sems, load_sems,
):
    tile = lax.axis_index("tile")
    front = lax.axis_index("front")
    rows, width = child_out.shape
    slab = prhs_ref.shape[0]
    parent_rows = plower.shape[1]
    border_total = ub.shape[1]
    border_own = border.shape[0]
    quarter_rows = parent_rows // 4

    def bit_of(axis, b):
        return ((tile if axis == "tile" else front) // (1 << b)) % 2

    def partner(axis, b):
        pos = tile if axis == "tile" else front
        return {axis: pos + (1 << b) * (1 - 2 * bit_of(axis, b))}

    child_dims = [("tile", b) for b in reversed(range(tile_bits))]
    parent_dims = [("front", 1), ("front", 0)] + child_dims

    loads = []
    pairs = (
        (rhs_hbm, rhs_buf.at[tuple(bit_of(*d) for d in child_dims)]),
        (ub_hbm, ub), (lower_hbm, lower), (border_hbm, border),
        (plower_hbm, plower), (pupper_hbm, pupper), (upper_hbm, upper),
    )
    for i, (src, dst) in enumerate(pairs):
        load = pltpu.make_async_copy(src, dst, load_sems.at[i])
        load.start()
        loads.append(load)

    barrier = pltpu.get_barrier_semaphore()
    for d in parent_dims:
        pl.semaphore_signal(
            barrier, inc=1, device_id=partner(*d), device_id_type=pl.DeviceIdType.MESH
        )
    pl.semaphore_wait(barrier, len(parent_dims))

    counter = [0]
    pending = []

    def send(src, dst, d):
        number = counter[0]
        counter[0] += 1
        copy = pltpu.make_async_remote_copy(
            src_ref=src, dst_ref=dst,
            send_sem=send_sems.at[number], recv_sem=recv_sems.at[number],
            device_id=partner(*d), device_id_type=pl.DeviceIdType.MESH,
        )
        copy.start()
        pending.append(copy)
        return copy

    def gather(buf, dims, orders, pieces, fill=None):
        last = [None] * len(pieces)
        held = [set() for _ in pieces]
        for step in range(len(dims)):
            for p, (start, size) in enumerate(pieces):
                if last[p] is not None:
                    last[p].wait_recv()
                d = orders[p][step]
                where = tuple(slice(None) if e in held[p] else bit_of(*e) for e in dims)
                view = buf.at[where + (pl.ds(start, size), slice(None))]
                last[p] = send(view, view, d)
                held[p].add(d)
            if fill is not None:
                fill(step)
        for copy in last:
            copy.wait_recv()

    child_pieces = cut_rows(rows, 2)
    child_orders = [rotate(child_dims[::-1], p * (tile_bits // 2)) for p in range(2)]
    parent_pieces = cut_rows(slab, 3)
    across = [d for d in parent_dims if d != ("front", 0)]
    rotated = [rotate(across, p * len(across) // 3) for p in range(3)]
    parent_orders = [r + [("front", 0)] for r in rotated]
    sum_orders = [[("front", 0)] + r for r in rotated]
    own_child = tuple(bit_of(*d) for d in child_dims)
    own_parent = tuple(bit_of(*d) for d in parent_dims)

    def child_product(matrix, buf, out):
        count = 1 << tile_bits

        def body(j, carry):
            where = tuple((j // (1 << b)) % 2 for _, b in child_dims)
            columns = pl.ds(pl.multiple_of(j * rows, rows), rows)
            term = dot3(split(matrix[:, columns]), split(buf[where]))

            @pl.when(j == 0)
            def _():
                out[...] = term

            @pl.when(j > 0)
            def _():
                out[...] += term

            return carry

        lax.fori_loop(0, count, body, 0)

    def quarter_of(buf, q):
        return buf[q // 2, q % 2].reshape(quarter_rows, width)

    def parent_product(matrix, buf):
        total = None
        for q in range(4):
            columns = slice(q * quarter_rows, (q + 1) * quarter_rows)
            term = dot3(split(matrix[:, columns]), split(quarter_of(buf, q)))
            total = term if total is None else total + term
        return total

    live = count_ref[0]
    chunk = 256
    chunks = parent_rows // chunk

    def permute_chunk(c):
        base = c * chunk
        lanes = lax.broadcasted_iota(jnp.int32, (1, border_total), 1)
        target = jnp.where(lanes < live, map_ref[...], -1) - base
        ids = lax.broadcasted_iota(jnp.int32, (chunk, border_total), 0)
        chosen = jnp.where(ids == target, 1.0, 0.0).astype(BF16)
        columns = pl.ds(pl.multiple_of(base, chunk), chunk)
        over = (((1,), (1,)), ((), ()))
        for source, result in ((ub_high, ubp_high), (ub_low, ubp_low)):
            result[:, columns] = lax.dot_general(
                source[...], chosen, over, preferred_element_type=F32
            ).astype(BF16)

    def permute(step):
        if step == 0:
            loads[1].wait()

            def body(i, carry):
                where = pl.ds(pl.multiple_of(i * 32, 32), 32)
                high, low = split(ub[where, :])
                ub_high[where, :] = high
                ub_low[where, :] = low
                return carry

            lax.fori_loop(0, rows // 32, body, 0)
        low = chunks * step // tile_bits
        top = chunks * (step + 1) // tile_bits

        def body(c, carry):
            permute_chunk(c)
            return carry

        lax.fori_loop(low, top, body, 0)

    loads[0].wait()
    gather(rhs_buf, child_dims, child_orders, child_pieces, permute)
    loads[2].wait()
    own_fc = fc_buf.at[own_child]
    child_product(lower, rhs_buf, own_fc)
    gather(fc_buf, child_dims, child_orders, child_pieces)
    loads[3].wait()
    child_product(border, fc_buf, child_out)

    start = pl.multiple_of(tile * border_own, border_own)
    lanes = start + lax.broadcasted_iota(jnp.int32, (1, border_own), 1)
    target = jnp.where(lanes < live, map_ref[:, pl.ds(start, border_own)], -1)
    high, low = split(child_out[...])
    for q in range(4):
        ids = q * quarter_rows + lax.broadcasted_iota(jnp.int32, (quarter_rows, border_own), 0)
        chosen = jnp.where(ids == target, 1.0, 0.0).astype(BF16)
        block = dot(chosen, high) + dot(chosen, low)
        part[q // 2, q % 2] = block.reshape(part.shape[2:])

    last = [None] * 3
    settled = [[] for _ in range(3)]

    def add_arrived(step, p):
        begin, size = parent_pieces[p]
        last[p].wait_recv()
        where = tuple(bit_of(*e) if e in settled[p] else slice(None) for e in parent_dims)
        where += (pl.ds(begin, size), slice(None))
        part[where] = part[where] + landing[(step,) + where]

    for step in range(len(parent_dims)):
        for p, (begin, size) in enumerate(parent_pieces):
            if step > 0:
                add_arrived(step - 1, p)
            d = sum_orders[p][step]
            where = tuple(
                bit_of(*e) if e in settled[p] else (1 - bit_of(*e) if e == d else slice(None))
                for e in parent_dims
            ) + (pl.ds(begin, size), slice(None))
            last[p] = send(part.at[where], landing.at[(step,) + where], d)
            settled[p].append(d)
    for p in range(3):
        add_arrived(len(parent_dims) - 1, p)

    p1[own_parent] = prhs_ref[...] - part[own_parent]
    gather(p1, parent_dims, parent_orders, parent_pieces)
    loads[4].wait()
    p2[own_parent] = parent_product(plower, p1)
    gather(p2, parent_dims, parent_orders, parent_pieces)
    loads[5].wait()
    solved = parent_product(pupper, p2)
    p3[own_parent] = solved
    parent_out[...] = solved
    gather(p3, parent_dims, parent_orders, parent_pieces)

    total = own_fc[...]
    for q in range(4):
        columns = slice(q * quarter_rows, (q + 1) * quarter_rows)
        pair = (ubp_high[:, columns], ubp_low[:, columns])
        total = total - dot3(pair, split(quarter_of(p3, q)))
    red_buf[own_child] = total
    gather(red_buf, child_dims, child_orders, child_pieces)
    loads[6].wait()
    child_product(upper, red_buf, child_out)
    for copy in pending:
        copy.wait_send()


def local(
    child_rhs, child_lower, child_border, child_upper_border, child_upper,
    parent_rhs, parent_lower, parent_upper, border_map, border_count,
):
    tiles = lax.axis_size("tile")
    tile_bits = tiles.bit_length() - 1
    rows, width = child_rhs.shape[1:]
    slab = parent_rhs.shape[1]
    child_shape = (2,) * tile_bits + (rows, width)
    parent_shape = (2,) * (tile_bits + 2) + (slab, width)
    steps = tile_bits + 2
    sends = 3 * 2 * tile_bits + 4 * 3 * steps
    vmem = pl.BlockSpec(memory_space=pltpu.VMEM)
    hbm = pl.BlockSpec(memory_space=pl.ANY)
    smem = pl.BlockSpec(memory_space=pltpu.SMEM)
    matrices = [child_lower, child_border, child_upper_border, child_upper, parent_lower, parent_upper]
    child_solution, solved = pl.pallas_call(
        functools.partial(kernel, tile_bits),
        out_shape=(
            jax.ShapeDtypeStruct((rows, width), F32),
            jax.ShapeDtypeStruct((slab, width), F32),
        ),
        in_specs=[hbm, hbm, hbm, hbm, hbm, vmem, hbm, hbm, vmem, smem],
        out_specs=(vmem, vmem),
        scratch_shapes=[pltpu.VMEM(child_shape, F32)] * 3
        + [pltpu.VMEM(parent_shape, F32)] * 4
        + [pltpu.VMEM((steps,) + parent_shape, F32)]
        + [pltpu.VMEM(m.shape[1:], F32) for m in matrices]
        + [pltpu.VMEM(child_upper_border.shape[1:], BF16)] * 2
        + [pltpu.VMEM((rows, parent_lower.shape[2]), BF16)] * 2
        + [
            pltpu.SemaphoreType.DMA((sends,)),
            pltpu.SemaphoreType.DMA((sends,)),
            pltpu.SemaphoreType.DMA((7,)),
        ],
        compiler_params=pltpu.CompilerParams(
            collective_id=0, has_side_effects=True, vmem_limit_bytes=60 << 20
        ),
    )(
        child_rhs[0], child_lower[0], child_border[0], child_upper_border[0], child_upper[0],
        parent_rhs[0], parent_lower[0], parent_upper[0], border_map, border_count,
    )
    return (child_solution[None], solved[None])


def solution(mesh):
    return jax.shard_map(
        local,
        mesh=mesh,
        in_specs=(
            P("front", "tile", None),
            P("front", "tile", None),
            P("front", "tile", None),
            P("front", "tile", None),
            P("front", "tile", None),
            P("front", "tile", None),
            P("front", "tile", None),
            P("front", "tile", None),
            P("front", None),
            P("front"),
        ),
        out_specs=(P("front", "tile", None), P("front", "tile", None)),
        check_vma=False,
    )
```

```python
import functools

import jax
import jax.numpy as jnp
from jax import lax
from jax.experimental import pallas as pl
from jax.experimental.pallas import tpu as pltpu
from jax.sharding import PartitionSpec as P

F32 = jnp.float32
BF16 = jnp.bfloat16


def split(x):
    high = x.astype(BF16)
    return high, (x - high.astype(F32)).astype(BF16)


def dot(a, b):
    return jnp.dot(a, b, preferred_element_type=F32)


def dot3(a, b):
    ah, al = a
    bh, bl = b
    return dot(ah, bh) + (dot(ah, bl) + dot(al, bh))


def cut_rows(rows, parts):
    units = rows // 8
    sizes = [8 * (units // parts + (1 if p < units % parts else 0)) for p in range(parts)]
    starts = [sum(sizes[:p]) for p in range(parts)]
    return list(zip(starts, sizes))


def rotate(items, by):
    by %= len(items)
    return items[by:] + items[:by]


def kernel(
    tile_bits,
    rhs_hbm, lower_hbm, border_hbm, ub_hbm, upper_hbm, prhs_ref, plower_hbm, pupper_hbm,
    map_ref, count_ref,
    child_out, parent_out,
    rhs_buf, fc_buf, red_buf, p1, p2, p3, part, landing,
    lower, border, ub, upper, plower, pupper, ub_high, ub_low, ubp_high, ubp_low,
    send_sems, recv_sems, load_sems,
):
    tile = lax.axis_index("tile")
    front = lax.axis_index("front")
    rows, width = child_out.shape
    slab = prhs_ref.shape[0]
    parent_rows = plower.shape[1]
    border_total = ub.shape[1]
    border_own = border.shape[0]
    quarter_rows = parent_rows // 4

    def bit_of(axis, b):
        return ((tile if axis == "tile" else front) // (1 << b)) % 2

    def partner(axis, b):
        pos = tile if axis == "tile" else front
        return {axis: pos + (1 << b) * (1 - 2 * bit_of(axis, b))}

    child_dims = [("tile", b) for b in reversed(range(tile_bits))]
    parent_dims = [("front", 1), ("front", 0)] + child_dims

    loads = []
    pairs = (
        (rhs_hbm, rhs_buf.at[tuple(bit_of(*d) for d in child_dims)]),
        (ub_hbm, ub), (lower_hbm, lower), (border_hbm, border),
        (plower_hbm, plower), (pupper_hbm, pupper), (upper_hbm, upper),
    )
    for i, (src, dst) in enumerate(pairs):
        load = pltpu.make_async_copy(src, dst, load_sems.at[i])
        load.start()
        loads.append(load)

    barrier = pltpu.get_barrier_semaphore()
    for d in parent_dims:
        pl.semaphore_signal(
            barrier, inc=1, device_id=partner(*d), device_id_type=pl.DeviceIdType.MESH
        )
    pl.semaphore_wait(barrier, len(parent_dims))

    counter = [0]
    pending = []

    def send(src, dst, d):
        number = counter[0]
        counter[0] += 1
        copy = pltpu.make_async_remote_copy(
            src_ref=src, dst_ref=dst,
            send_sem=send_sems.at[number], recv_sem=recv_sems.at[number],
            device_id=partner(*d), device_id_type=pl.DeviceIdType.MESH,
        )
        copy.start()
        pending.append(copy)
        return copy

    def gather(buf, dims, orders, pieces, fill=None):
        last = [None] * len(pieces)
        held = [set() for _ in pieces]
        for step in range(len(dims)):
            for p, (start, size) in enumerate(pieces):
                if last[p] is not None:
                    last[p].wait_recv()
                d = orders[p][step]
                where = tuple(slice(None) if e in held[p] else bit_of(*e) for e in dims)
                view = buf.at[where + (pl.ds(start, size), slice(None))]
                last[p] = send(view, view, d)
                held[p].add(d)
            if fill is not None:
                fill(step)
        for copy in last:
            copy.wait_recv()

    def flood(buf, dims, orders, pieces):
        depth = len(dims)
        paths = [
            tuple(i for i in range(depth) if m >> i & 1) for m in range(1, 1 << depth)
        ]
        copies = {}

        def launch(p, path):
            start, size = pieces[p]
            flipped = [orders[p][i] for i in path[:-1]]
            where = tuple(1 - bit_of(*e) if e in flipped else bit_of(*e) for e in dims)
            view = buf.at[where + (pl.ds(start, size), slice(None))]
            copies[p, path] = send(view, view, orders[p][path[-1]])

        def wait(p, path):
            copies[p, path].wait_recv()
            for i in range(path[-1] + 1, depth):
                launch(p, path + (i,))

        for i in range(depth):
            for p in range(len(pieces)):
                launch(p, (i,))
        return paths, wait

    def gather_parent(buf):
        if tile_bits > 2:
            gather(buf, parent_dims, parent_orders, parent_pieces)
            return
        paths, wait = flood(buf, parent_dims, parent_orders, parent_pieces)
        for path in sorted(paths, key=lambda path: (len(path), path)):
            for p in range(3):
                wait(p, path)

    def apply_child(matrix, buf, out, load, fill=None):
        if tile_bits > 2:
            gather(buf, child_dims, child_orders, child_pieces, fill)
            load.wait()
            child_product(matrix, buf, out)
            return
        paths, wait = flood(buf, child_dims, child_orders, child_pieces)

        def use(flips, first=False):
            where = tuple(1 - bit_of(*e) if e in flips else bit_of(*e) for e in child_dims)
            j = sum(w * (1 << b) for w, (_, b) in zip(where, child_dims))
            columns = pl.ds(pl.multiple_of(j * rows, rows), rows)
            term = dot3(split(matrix[:, columns]), split(buf[where]))
            if first:
                out[...] = term
            else:
                out[...] += term

        if fill is not None:
            fill(0)
        load.wait()
        use((), True)
        wait(0, (0,))
        wait(1, (0,))
        if fill is not None:
            fill(1)
        wait(0, (1,))
        wait(1, (1,))
        use(child_dims[:1])
        use(child_dims[1:])
        wait(0, (0, 1))
        wait(1, (0, 1))
        use(child_dims)

    child_pieces = cut_rows(rows, 2)
    child_orders = [rotate(child_dims[::-1], p * (tile_bits // 2)) for p in range(2)]
    parent_pieces = cut_rows(slab, 3)
    across = [d for d in parent_dims if d != ("front", 0)]
    rotated = [rotate(across, p * len(across) // 3) for p in range(3)]
    parent_orders = [r + [("front", 0)] for r in rotated]
    sum_orders = [[("front", 0)] + r for r in rotated]
    own_child = tuple(bit_of(*d) for d in child_dims)
    own_parent = tuple(bit_of(*d) for d in parent_dims)

    def child_product(matrix, buf, out):
        count = 1 << tile_bits

        def body(j, carry):
            where = tuple((j // (1 << b)) % 2 for _, b in child_dims)
            columns = pl.ds(pl.multiple_of(j * rows, rows), rows)
            term = dot3(split(matrix[:, columns]), split(buf[where]))

            @pl.when(j == 0)
            def _():
                out[...] = term

            @pl.when(j > 0)
            def _():
                out[...] += term

            return carry

        lax.fori_loop(0, count, body, 0)

    def quarter_of(buf, q):
        return buf[q // 2, q % 2].reshape(quarter_rows, width)

    def parent_product(matrix, buf):
        total = None
        for q in range(4):
            columns = slice(q * quarter_rows, (q + 1) * quarter_rows)
            term = dot3(split(matrix[:, columns]), split(quarter_of(buf, q)))
            total = term if total is None else total + term
        return total

    live = count_ref[0]
    chunk = 256
    chunks = parent_rows // chunk

    def permute_chunk(c):
        base = c * chunk
        lanes = lax.broadcasted_iota(jnp.int32, (1, border_total), 1)
        target = jnp.where(lanes < live, map_ref[...], -1) - base
        ids = lax.broadcasted_iota(jnp.int32, (chunk, border_total), 0)
        chosen = jnp.where(ids == target, 1.0, 0.0).astype(BF16)
        columns = pl.ds(pl.multiple_of(base, chunk), chunk)
        over = (((1,), (1,)), ((), ()))
        for source, result in ((ub_high, ubp_high), (ub_low, ubp_low)):
            result[:, columns] = lax.dot_general(
                source[...], chosen, over, preferred_element_type=F32
            ).astype(BF16)

    def permute(step):
        if step == 0:
            loads[1].wait()

            def body(i, carry):
                where = pl.ds(pl.multiple_of(i * 32, 32), 32)
                high, low = split(ub[where, :])
                ub_high[where, :] = high
                ub_low[where, :] = low
                return carry

            lax.fori_loop(0, rows // 32, body, 0)
        low = chunks * step // tile_bits
        top = chunks * (step + 1) // tile_bits

        def body(c, carry):
            permute_chunk(c)
            return carry

        lax.fori_loop(low, top, body, 0)

    loads[0].wait()
    own_fc = fc_buf.at[own_child]
    apply_child(lower, rhs_buf, own_fc, loads[2], permute)
    apply_child(border, fc_buf, child_out, loads[3])

    start = pl.multiple_of(tile * border_own, border_own)
    lanes = start + lax.broadcasted_iota(jnp.int32, (1, border_own), 1)
    target = jnp.where(lanes < live, map_ref[:, pl.ds(start, border_own)], -1)
    high, low = split(child_out[...])
    core = bit_of("front", 0)

    def contributions(high_bit, low_bit):
        q = high_bit * 2 + low_bit
        ids = q * quarter_rows + lax.broadcasted_iota(jnp.int32, (quarter_rows, border_own), 0)
        chosen = jnp.where(ids == target, 1.0, 0.0).astype(BF16)
        block = dot(chosen, high) + dot(chosen, low)
        part[high_bit, low_bit] = block.reshape(part.shape[2:])

    handed = []
    for high_bit in range(2):
        contributions(high_bit, 1 - core)
        handed.append(
            send(part.at[high_bit, 1 - core], landing.at[0, high_bit, 1 - core], ("front", 0))
        )
    for high_bit in range(2):
        contributions(high_bit, core)
    for high_bit in range(2):
        handed[high_bit].wait_recv()
        part[high_bit, core] = part[high_bit, core] + landing[0, high_bit, core]

    last = [None] * 3
    settled = [[("front", 0)] for _ in range(3)]

    def add_arrived(step, p):
        begin, size = parent_pieces[p]
        last[p].wait_recv()
        where = tuple(bit_of(*e) if e in settled[p] else slice(None) for e in parent_dims)
        where += (pl.ds(begin, size), slice(None))
        part[where] = part[where] + landing[(step,) + where]

    for step in range(1, len(parent_dims)):
        for p, (begin, size) in enumerate(parent_pieces):
            if step > 1:
                add_arrived(step - 1, p)
            d = sum_orders[p][step]
            where = tuple(
                bit_of(*e) if e in settled[p] else (1 - bit_of(*e) if e == d else slice(None))
                for e in parent_dims
            ) + (pl.ds(begin, size), slice(None))
            last[p] = send(part.at[where], landing.at[(step,) + where], d)
            settled[p].append(d)
    for p in range(3):
        add_arrived(len(parent_dims) - 1, p)

    p1[own_parent] = prhs_ref[...] - part[own_parent]
    gather_parent(p1)
    loads[4].wait()
    p2[own_parent] = parent_product(plower, p1)
    gather_parent(p2)
    loads[5].wait()
    solved = parent_product(pupper, p2)
    p3[own_parent] = solved
    parent_out[...] = solved
    gather_parent(p3)

    total = own_fc[...]
    for q in range(4):
        columns = slice(q * quarter_rows, (q + 1) * quarter_rows)
        pair = (ubp_high[:, columns], ubp_low[:, columns])
        total = total - dot3(pair, split(quarter_of(p3, q)))
    red_buf[own_child] = total
    apply_child(upper, red_buf, child_out, loads[6])
    for copy in pending:
        copy.wait_send()


def local(
    child_rhs, child_lower, child_border, child_upper_border, child_upper,
    parent_rhs, parent_lower, parent_upper, border_map, border_count,
):
    tiles = lax.axis_size("tile")
    tile_bits = tiles.bit_length() - 1
    rows, width = child_rhs.shape[1:]
    slab = parent_rhs.shape[1]
    child_shape = (2,) * tile_bits + (rows, width)
    parent_shape = (2,) * (tile_bits + 2) + (slab, width)
    steps = tile_bits + 2
    sends = 3 * 2 * tile_bits + 4 * 3 * steps
    if tile_bits <= 2:
        sends = 3 * 2 * (tiles - 1) + 3 * 3 * (4 * tiles - 1) + 3 * steps
    vmem = pl.BlockSpec(memory_space=pltpu.VMEM)
    hbm = pl.BlockSpec(memory_space=pl.ANY)
    smem = pl.BlockSpec(memory_space=pltpu.SMEM)
    matrices = [child_lower, child_border, child_upper_border, child_upper, parent_lower, parent_upper]
    child_solution, solved = pl.pallas_call(
        functools.partial(kernel, tile_bits),
        out_shape=(
            jax.ShapeDtypeStruct((rows, width), F32),
            jax.ShapeDtypeStruct((slab, width), F32),
        ),
        in_specs=[hbm, hbm, hbm, hbm, hbm, vmem, hbm, hbm, vmem, smem],
        out_specs=(vmem, vmem),
        scratch_shapes=[pltpu.VMEM(child_shape, F32)] * 3
        + [pltpu.VMEM(parent_shape, F32)] * 4
        + [pltpu.VMEM((steps,) + parent_shape, F32)]
        + [pltpu.VMEM(m.shape[1:], F32) for m in matrices]
        + [pltpu.VMEM(child_upper_border.shape[1:], BF16)] * 2
        + [pltpu.VMEM((rows, parent_lower.shape[2]), BF16)] * 2
        + [
            pltpu.SemaphoreType.DMA((sends,)),
            pltpu.SemaphoreType.DMA((sends,)),
            pltpu.SemaphoreType.DMA((7,)),
        ],
        compiler_params=pltpu.CompilerParams(
            collective_id=0, has_side_effects=True, vmem_limit_bytes=60 << 20
        ),
    )(
        child_rhs[0], child_lower[0], child_border[0], child_upper_border[0], child_upper[0],
        parent_rhs[0], parent_lower[0], parent_upper[0], border_map, border_count,
    )
    return (child_solution[None], solved[None])


def solution(mesh):
    return jax.shard_map(
        local,
        mesh=mesh,
        in_specs=(
            P("front", "tile", None),
            P("front", "tile", None),
            P("front", "tile", None),
            P("front", "tile", None),
            P("front", "tile", None),
            P("front", "tile", None),
            P("front", "tile", None),
            P("front", "tile", None),
            P("front", None),
            P("front"),
        ),
        out_specs=(P("front", "tile", None), P("front", "tile", None)),
        check_vma=False,
    )
```

```python
import functools

import jax
import jax.numpy as jnp
from jax import lax
from jax.experimental import pallas as pl
from jax.experimental.pallas import tpu as pltpu
from jax.sharding import PartitionSpec as P

F32 = jnp.float32
BF16 = jnp.bfloat16


def split(x):
    high = x.astype(BF16)
    return high, (x - high.astype(F32)).astype(BF16)


def dot(a, b):
    return jnp.dot(a, b, preferred_element_type=F32)


def dot3(a, b):
    ah, al = a
    bh, bl = b
    return dot(ah, bh) + (dot(ah, bl) + dot(al, bh))


def cut_rows(rows, parts):
    units = rows // 8
    sizes = [8 * (units // parts + (1 if p < units % parts else 0)) for p in range(parts)]
    starts = [sum(sizes[:p]) for p in range(parts)]
    return list(zip(starts, sizes))


def rotate(items, by):
    by %= len(items)
    return items[by:] + items[:by]


def kernel(
    tile_bits,
    rhs_hbm, lower_hbm, border_hbm, ub_hbm, upper_hbm, prhs_hbm, plower_hbm, pupper_hbm,
    map_hbm, count_hbm,
    child_out, parent_hbm,
    rhs_buf, fc_buf, red_buf, p1, p2, p3, part, landing,
    lower, border, ub, upper, plower, pupper, ub_high, ub_low, ubp_high, ubp_low,
    prhs_ref, map_ref, count_ref, parent_out,
    send_sems, recv_sems, load_sems,
):
    tile = lax.axis_index("tile")
    front = lax.axis_index("front")
    rows, width = child_out.shape
    slab = prhs_ref.shape[0]
    parent_rows = plower.shape[1]
    border_total = ub.shape[1]
    border_own = border.shape[0]
    quarter_rows = parent_rows // 4

    def bit_of(axis, b):
        return ((tile if axis == "tile" else front) // (1 << b)) % 2

    def partner(axis, b):
        pos = tile if axis == "tile" else front
        return {axis: pos + (1 << b) * (1 - 2 * bit_of(axis, b))}

    child_dims = [("tile", b) for b in reversed(range(tile_bits))]
    parent_dims = [("front", 1), ("front", 0)] + child_dims

    loads = []
    pairs = (
        (rhs_hbm, rhs_buf.at[tuple(bit_of(*d) for d in child_dims)]),
        (ub_hbm, ub), (lower_hbm, lower), (border_hbm, border),
        (plower_hbm, plower), (pupper_hbm, pupper), (upper_hbm, upper),
        (map_hbm, map_ref), (count_hbm, count_ref), (prhs_hbm, prhs_ref),
    )
    for i, (src, dst) in enumerate(pairs):
        load = pltpu.make_async_copy(src, dst, load_sems.at[i])
        loads.append(load)
    loads[0].start()

    barrier = pltpu.get_barrier_semaphore()
    for d in parent_dims:
        pl.semaphore_signal(
            barrier, inc=1, device_id=partner(*d), device_id_type=pl.DeviceIdType.MESH
        )
    pl.semaphore_wait(barrier, len(parent_dims))

    counter = [0]
    pending = []

    def send(src, dst, d):
        number = counter[0]
        counter[0] += 1
        copy = pltpu.make_async_remote_copy(
            src_ref=src, dst_ref=dst,
            send_sem=send_sems.at[number], recv_sem=recv_sems.at[number],
            device_id=partner(*d), device_id_type=pl.DeviceIdType.MESH,
        )
        copy.start()
        pending.append(copy)
        return copy

    def gather(buf, dims, orders, pieces, fill=None):
        last = [None] * len(pieces)
        held = [set() for _ in pieces]
        for step in range(len(dims)):
            for p, (start, size) in enumerate(pieces):
                if last[p] is not None:
                    last[p].wait_recv()
                d = orders[p][step]
                where = tuple(slice(None) if e in held[p] else bit_of(*e) for e in dims)
                view = buf.at[where + (pl.ds(start, size), slice(None))]
                last[p] = send(view, view, d)
                held[p].add(d)
            if fill is not None:
                fill(step)
        for copy in last:
            copy.wait_recv()

    def flood(buf, dims, orders, pieces):
        depth = len(dims)
        paths = [
            tuple(i for i in range(depth) if m >> i & 1) for m in range(1, 1 << depth)
        ]
        copies = {}

        def launch(p, path):
            start, size = pieces[p]
            flipped = [orders[p][i] for i in path[:-1]]
            where = tuple(1 - bit_of(*e) if e in flipped else bit_of(*e) for e in dims)
            view = buf.at[where + (pl.ds(start, size), slice(None))]
            copies[p, path] = send(view, view, orders[p][path[-1]])

        def wait(p, path):
            copies[p, path].wait_recv()
            for i in range(path[-1] + 1, depth):
                launch(p, path + (i,))

        for i in range(depth):
            for p in range(len(pieces)):
                launch(p, (i,))
        return paths, wait

    def gather_parent(buf):
        if tile_bits > 2:
            gather(buf, parent_dims, parent_orders, parent_pieces)
            return
        paths, wait = flood(buf, parent_dims, parent_orders, parent_pieces)
        for path in sorted(paths, key=lambda path: (len(path), path)):
            for p in range(3):
                wait(p, path)

    def apply_child(matrix, buf, out, load, fill=None):
        if tile_bits > 2:
            gather(buf, child_dims, child_orders, child_pieces, fill)
            load.wait()
            child_product(matrix, buf, out)
            return
        paths, wait = flood(buf, child_dims, child_orders, child_pieces)

        def use(flips, first=False):
            where = tuple(1 - bit_of(*e) if e in flips else bit_of(*e) for e in child_dims)
            j = sum(w * (1 << b) for w, (_, b) in zip(where, child_dims))
            columns = pl.ds(pl.multiple_of(j * rows, rows), rows)
            term = dot3(split(matrix[:, columns]), split(buf[where]))
            if first:
                out[...] = term
            else:
                out[...] += term

        if fill is not None:
            fill(0)
        load.wait()
        use((), True)
        wait(0, (0,))
        wait(1, (0,))
        if fill is not None:
            fill(1)
        wait(0, (1,))
        wait(1, (1,))
        use(child_dims[:1])
        use(child_dims[1:])
        wait(0, (0, 1))
        wait(1, (0, 1))
        use(child_dims)

    child_pieces = cut_rows(rows, 2)
    child_orders = [rotate(child_dims[::-1], p * (tile_bits // 2)) for p in range(2)]
    parent_pieces = cut_rows(slab, 3)
    across = [d for d in parent_dims if d != ("front", 0)]
    rotated = [rotate(across, p * len(across) // 3) for p in range(3)]
    parent_orders = [r + [("front", 0)] for r in rotated]
    sum_pieces = cut_rows(slab, 6 if tile_bits <= 2 else 3)
    sum_orders = [[("front", 0)] + rotated[p % 3] for p in range(len(sum_pieces))]
    own_child = tuple(bit_of(*d) for d in child_dims)
    own_parent = tuple(bit_of(*d) for d in parent_dims)

    def child_product(matrix, buf, out):
        count = 1 << tile_bits

        def body(j, carry):
            where = tuple((j // (1 << b)) % 2 for _, b in child_dims)
            columns = pl.ds(pl.multiple_of(j * rows, rows), rows)
            term = dot3(split(matrix[:, columns]), split(buf[where]))

            @pl.when(j == 0)
            def _():
                out[...] = term

            @pl.when(j > 0)
            def _():
                out[...] += term

            return carry

        lax.fori_loop(0, count, body, 0)

    def quarter_of(buf, q):
        return buf[q // 2, q % 2].reshape(quarter_rows, width)

    def parent_product(matrix, buf):
        total = None
        for q in range(4):
            columns = slice(q * quarter_rows, (q + 1) * quarter_rows)
            term = dot3(split(matrix[:, columns]), split(quarter_of(buf, q)))
            total = term if total is None else total + term
        return total

    chunk = 256
    chunks = parent_rows // chunk

    def permute_chunk(c):
        base = c * chunk
        lanes = lax.broadcasted_iota(jnp.int32, (1, border_total), 1)
        target = jnp.where(lanes < count_ref[0], map_ref[...], -1) - base
        ids = lax.broadcasted_iota(jnp.int32, (chunk, border_total), 0)
        chosen = jnp.where(ids == target, 1.0, 0.0).astype(BF16)
        columns = pl.ds(pl.multiple_of(base, chunk), chunk)
        over = (((1,), (1,)), ((), ()))
        for source, result in ((ub_high, ubp_high), (ub_low, ubp_low)):
            result[:, columns] = lax.dot_general(
                source[...], chosen, over, preferred_element_type=F32
            ).astype(BF16)

    shares = ((0, 1, 2), (2, 5, 8))

    def permute(turn, step):
        if step > 1:
            return
        if turn == 0 and step == 0:
            for i in (7, 8, 2, 1, 3, 9, 4, 5, 6):
                loads[i].start()
            for i in (7, 8, 1):
                loads[i].wait()

            def body(i, carry):
                where = pl.ds(pl.multiple_of(i * 32, 32), 32)
                high, low = split(ub[where, :])
                ub_high[where, :] = high
                ub_low[where, :] = low
                return carry

            lax.fori_loop(0, rows // 32, body, 0)
        low = chunks * shares[turn][step] // 8
        top = chunks * shares[turn][step + 1] // 8

        def body(c, carry):
            permute_chunk(c)
            return carry

        lax.fori_loop(low, top, body, 0)

    loads[0].wait()
    own_fc = fc_buf.at[own_child]
    apply_child(lower, rhs_buf, own_fc, loads[2], functools.partial(permute, 0))
    apply_child(border, fc_buf, child_out, loads[3], functools.partial(permute, 1))

    start = pl.multiple_of(tile * border_own, border_own)
    lanes = start + lax.broadcasted_iota(jnp.int32, (1, border_own), 1)
    target = jnp.where(lanes < count_ref[0], map_ref[:, pl.ds(start, border_own)], -1)
    high, low = split(child_out[...])
    core = bit_of("front", 0)

    def contributions(high_bit, low_bit):
        q = high_bit * 2 + low_bit
        ids = q * quarter_rows + lax.broadcasted_iota(jnp.int32, (quarter_rows, border_own), 0)
        chosen = jnp.where(ids == target, 1.0, 0.0).astype(BF16)
        block = dot(chosen, high) + dot(chosen, low)
        part[high_bit, low_bit] = block.reshape(part.shape[2:])

    far = 1 - bit_of("front", 1)
    handed = []
    for high_bit in (far, 1 - far):
        contributions(high_bit, 1 - core)
        handed.append(
            send(part.at[high_bit, 1 - core], landing.at[0, high_bit, 1 - core], ("front", 0))
        )
    for high_bit in (far, 1 - far):
        contributions(high_bit, core)
    for copy, high_bit in zip(handed, (far, 1 - far)):
        copy.wait_recv()
        part[high_bit, core] = part[high_bit, core] + landing[0, high_bit, core]

    last = [None] * len(sum_pieces)
    settled = [[("front", 0)] for _ in sum_pieces]

    def add_arrived(step, p):
        begin, size = sum_pieces[p]
        last[p].wait_recv()
        where = tuple(bit_of(*e) if e in settled[p] else slice(None) for e in parent_dims)
        where += (pl.ds(begin, size), slice(None))
        part[where] = part[where] + landing[(step,) + where]

    for step in range(1, len(parent_dims)):
        for p, (begin, size) in enumerate(sum_pieces):
            if step > 1:
                add_arrived(step - 1, p)
            d = sum_orders[p][step]
            where = tuple(
                bit_of(*e) if e in settled[p] else (1 - bit_of(*e) if e == d else slice(None))
                for e in parent_dims
            ) + (pl.ds(begin, size), slice(None))
            last[p] = send(part.at[where], landing.at[(step,) + where], d)
            settled[p].append(d)
    for p in range(len(sum_pieces)):
        add_arrived(len(parent_dims) - 1, p)

    loads[9].wait()
    p1[own_parent] = prhs_ref[...] - part[own_parent]
    gather_parent(p1)
    loads[4].wait()
    p2[own_parent] = parent_product(plower, p1)
    gather_parent(p2)
    loads[5].wait()
    solved = parent_product(pupper, p2)
    p3[own_parent] = solved
    parent_out[...] = solved
    leaving = pltpu.make_async_copy(parent_out, parent_hbm, load_sems.at[10])
    leaving.start()
    gather_parent(p3)
    leaving.wait()

    total = own_fc[...]
    for q in range(4):
        columns = slice(q * quarter_rows, (q + 1) * quarter_rows)
        pair = (ubp_high[:, columns], ubp_low[:, columns])
        total = total - dot3(pair, split(quarter_of(p3, q)))
    red_buf[own_child] = total
    apply_child(upper, red_buf, child_out, loads[6])
    for copy in pending:
        copy.wait_send()


def local(
    child_rhs, child_lower, child_border, child_upper_border, child_upper,
    parent_rhs, parent_lower, parent_upper, border_map, border_count,
):
    tiles = lax.axis_size("tile")
    tile_bits = tiles.bit_length() - 1
    rows, width = child_rhs.shape[1:]
    slab = parent_rhs.shape[1]
    child_shape = (2,) * tile_bits + (rows, width)
    parent_shape = (2,) * (tile_bits + 2) + (slab, width)
    steps = tile_bits + 2
    sends = 3 * 2 * tile_bits + 4 * 3 * steps
    if tile_bits <= 2:
        sends = 3 * 2 * (tiles - 1) + 3 * 3 * (4 * tiles - 1) + 6 * steps
    vmem = pl.BlockSpec(memory_space=pltpu.VMEM)
    hbm = pl.BlockSpec(memory_space=pl.ANY)
    matrices = [child_lower, child_border, child_upper_border, child_upper, parent_lower, parent_upper]
    child_solution, solved = pl.pallas_call(
        functools.partial(kernel, tile_bits),
        out_shape=(
            jax.ShapeDtypeStruct((rows, width), F32),
            jax.ShapeDtypeStruct((slab, width), F32),
        ),
        in_specs=[hbm] * 10,
        out_specs=(vmem, hbm),
        scratch_shapes=[pltpu.VMEM(child_shape, F32)] * 3
        + [pltpu.VMEM(parent_shape, F32)] * 4
        + [pltpu.VMEM((steps,) + parent_shape, F32)]
        + [pltpu.VMEM(m.shape[1:], F32) for m in matrices]
        + [pltpu.VMEM(child_upper_border.shape[1:], BF16)] * 2
        + [pltpu.VMEM((rows, parent_lower.shape[2]), BF16)] * 2
        + [
            pltpu.VMEM((slab, width), F32),
            pltpu.VMEM(border_map.shape, jnp.int32),
            pltpu.SMEM(border_count.shape, jnp.int32),
            pltpu.VMEM((slab, width), F32),
            pltpu.SemaphoreType.DMA((sends,)),
            pltpu.SemaphoreType.DMA((sends,)),
            pltpu.SemaphoreType.DMA((11,)),
        ],
        compiler_params=pltpu.CompilerParams(
            collective_id=0, has_side_effects=True, vmem_limit_bytes=60 << 20
        ),
    )(
        child_rhs[0], child_lower[0], child_border[0], child_upper_border[0], child_upper[0],
        parent_rhs[0], parent_lower[0], parent_upper[0], border_map, border_count,
    )
    return (child_solution[None], solved[None])


def solution(mesh):
    return jax.shard_map(
        local,
        mesh=mesh,
        in_specs=(
            P("front", "tile", None),
            P("front", "tile", None),
            P("front", "tile", None),
            P("front", "tile", None),
            P("front", "tile", None),
            P("front", "tile", None),
            P("front", "tile", None),
            P("front", "tile", None),
            P("front", None),
            P("front"),
        ),
        out_specs=(P("front", "tile", None), P("front", "tile", None)),
        check_vma=False,
    )
```
